32 devices in a mesh: sp: 8 (over z, y), ch: 4 (over x, core).
Axes of the slice: x: 2, y: 2, z: 4, core: 2. Of those that a mesh axis runs over, the one named last changes fastest.
Arguments:
- inputs: bfloat16 [2, 256, 1024, 1024], P(None, 'ch', 'sp'), may hold values from -6 to 6
- cotangent: bfloat16 [2, 256, 1024, 1024], P(None, 'ch', 'sp'), may hold values from -6 to 6
- input_factor: bfloat16 [256, 26], P('ch'), may hold values from -0.375 to 0.375
- output_factor: bfloat16 [256, 26], P('ch'), may hold values from -0.375 to 0.375
- height_factor: float32 [96, 10], replicated, may hold values from -0.625 to 0.625
- width_factor: float32 [96, 10], replicated, may hold values from -0.625 to 0.625
- core_tensor: float32 [2, 26, 26, 10, 10], replicated, may hold values from -0.078125 to 0.078125
Outputs:
- core_grad: float32 [2, 26, 26, 10, 10], replicated
- input_grad: float32 [256, 26], P('ch')
- output_grad: float32 [256, 26], P('ch')
- height_grad: float32 [96, 10], replicated
- width_grad: float32 [96, 10], replicated
The draws below stay inside these ranges and needn't reach their ends.
All inputs are finite; a program needn't handle non-finite values.
Results may differ from the reference program's by a relative error of at most 0.0086.
Values may be sent and summed in bfloat16 or wider, within the bound.
No kernel may reach another device: no remote copies, remote signals or barrier semaphores. Data moves between devices by JAX's collectives and lax.ppermute only.
A program may use at most 448 MiB of HBM per device.

```python
import math
import jax
import jax.numpy as jnp
from jax import lax

B = 2
C = 256
H = 1024
W = 1024
K = 96
L = 96
R_IN = 26
R_OUT = 26
R_X = 10
R_Y = 10


def level_of(own_key, extent, cuts, smallest, largest):
    def one(dim, parts):
        draws = jax.random.uniform(jax.random.fold_in(jax.random.fold_in(own_key, 6), dim), (parts,), jnp.float32, smallest / len(cuts), largest / len(cuts))
        return jnp.repeat(jnp.exp(draws), extent[dim] // parts).reshape((-1,) + (1,) * (len(extent) - dim - 1))

    level = one(*cuts[0])
    for cut in cuts[1:]:
        level = level * one(*cut)
    return level


def noise(key, shape, scale, reach, cuts=(), held_as=jnp.bfloat16):
    values = jax.random.normal(key, shape, jnp.float32) * scale
    if len(cuts) > 0:
        values = level_of(key, shape, cuts, -0.22, 0.18) * values
    return jnp.clip(values, min=-reach, max=reach).astype(held_as)


def setup_inputs(seed: int = 0) -> dict:
    arg_keys = jax.random.split(jax.random.key(seed), 8)
    inputs = noise(arg_keys[0], (B, C, H, W), 1.0, 6.0, ((1, 4), (2, 8)))
    cotangent = noise(arg_keys[1], (B, C, H, W), 1.0, 6.0, ((1, 4), (2, 8)))
    input_factor = noise(arg_keys[2], (C, R_IN), C ** -0.5, 0.375, ((0, 4),))
    output_factor = noise(arg_keys[3], (C, R_OUT), C ** -0.5, 0.375, ((0, 4),))
    height_factor = noise(arg_keys[4], (K, R_X), K ** -0.5, 0.625, (), jnp.float32)
    width_factor = noise(arg_keys[5], (L, R_Y), L ** -0.5, 0.625, (), jnp.float32)
    core_tensor = noise(arg_keys[6], (2, R_IN, R_OUT, R_X, R_Y), (R_IN * R_OUT * R_X) ** -0.5, 0.078125, (), jnp.float32)
    return {"inputs": inputs, "cotangent": cotangent, "input_factor": input_factor, "output_factor": output_factor, "height_factor": height_factor, "width_factor": width_factor, "core_tensor": core_tensor}


precise = lax.Precision.HIGHEST

def product(form, *operands):
    return jnp.einsum(form, *operands, precision=precise)

def row_table(width, modes):
    columns = jnp.arange(width, dtype=jnp.int32)[:, None]
    frequency = jnp.arange(modes, dtype=jnp.int32)[None, :]
    phases = (columns * frequency % width).astype(jnp.float32)
    angles = phases * (2.0 * math.pi / width)
    scaling = 1.0 / math.sqrt(width)
    cosine = jnp.cos(angles) * scaling
    minus_sine = -jnp.sin(angles) * scaling
    return jnp.stack([cosine, minus_sine], axis=1).astype(jnp.bfloat16)

def column_table(height, kept):
    halfway = kept // 2
    ordinal = jnp.arange(kept, dtype=jnp.int32)
    frequency = jnp.where(ordinal < halfway, ordinal, ordinal + (height - kept))
    heights = jnp.arange(height, dtype=jnp.int32)
    phases = (frequency[:, None] * heights[None, :] % height).astype(jnp.float32)
    angles = phases * (2.0 * math.pi / height)
    scaling = 1.0 / math.sqrt(height)
    cosine = jnp.cos(angles) * scaling
    sines = jnp.sin(angles) * scaling
    upper = jnp.concatenate([cosine, sines], axis=1)
    lower = jnp.concatenate([-sines, cosine], axis=1)
    return jnp.concatenate([upper, lower], axis=0).astype(jnp.bfloat16)

def spectrum(field, row_weights, column_weights):
    samples, channels, height, width = field.shape
    flat = field.reshape(samples * channels, height, width)

    def single(one_plane):
        row_parts = jnp.einsum('hw,wpl->phl', one_plane, row_weights, preferred_element_type=jnp.float32).astype(jnp.bfloat16)
        stacked = row_parts.reshape(2 * height, row_parts.shape[2])
        return jnp.dot(column_weights, stacked, preferred_element_type=jnp.float32).astype(jnp.bfloat16)
    result = lax.map(single, flat)
    return result.reshape(samples, channels, 2, result.shape[1] // 2, result.shape[2])

def rounded(value):
    return lax.optimization_barrier(value.astype(jnp.bfloat16)).astype(jnp.float32)

def reference(inputs, cotangent, input_factor, output_factor, height_factor, width_factor, core_tensor):
    row_weights = row_table(W, L)
    column_weights = column_table(H, K)
    spec_input = spectrum(inputs, row_weights, column_weights).astype(jnp.float32)
    spec_cot = spectrum(cotangent, row_weights, column_weights).astype(jnp.float32)
    left = product('bipkl,ia->bapkl', spec_input, input_factor.astype(jnp.float32))
    right = product('bopkl,oe->bepkl', spec_cot, output_factor.astype(jnp.float32))
    left_real = left[:, :, 0]
    left_imag = -left[:, :, 1]
    right_real = right[:, :, 0]
    right_imag = right[:, :, 1]
    pair_real = product('bakl,bekl->aekl', left_real, right_real) - product('bakl,bekl->aekl', left_imag, right_imag)
    pair_imag = product('bakl,bekl->aekl', left_real, right_imag) + product('bakl,bekl->aekl', left_imag, right_real)
    core_real = core_tensor[0]
    core_imag = core_tensor[1]
    folded_real = product('aecd,ld->aecl', core_real, width_factor)
    folded_imag = product('aecd,ld->aecl', core_imag, width_factor)
    turned_real = product('aecd,kc->aedk', core_real, height_factor)
    turned_imag = product('aecd,kc->aedk', core_imag, height_factor)
    modal_real = product('aecl,kc->aekl', folded_real, height_factor)
    modal_imag = product('aecl,kc->aekl', folded_imag, height_factor)
    core_grad = jnp.stack([product('aekl,kc,ld->aecd', pair_real, height_factor, width_factor), product('aekl,kc,ld->aecd', pair_imag, height_factor, width_factor)], axis=0)
    height_grad = product('aekl,aecl->kc', pair_real, folded_real) + product('aekl,aecl->kc', pair_imag, folded_imag)
    width_grad = product('aekl,aedk->ld', pair_real, turned_real) + product('aekl,aedk->ld', pair_imag, turned_imag)
    inward_real = rounded(product('aekl,bekl->bakl', modal_real, right_real) + product('aekl,bekl->bakl', modal_imag, right_imag))
    inward_imag = rounded(product('aekl,bekl->bakl', modal_real, right_imag) - product('aekl,bekl->bakl', modal_imag, right_real))
    outward_real = rounded(product('aekl,bakl->bekl', modal_real, left_real) + product('aekl,bakl->bekl', modal_imag, left_imag))
    outward_imag = rounded(product('aekl,bakl->bekl', modal_real, left_imag) - product('aekl,bakl->bekl', modal_imag, left_real))
    input_grad = product('bikl,bakl->ia', spec_input[:, :, 0], inward_real) + product('bikl,bakl->ia', spec_input[:, :, 1], inward_imag)
    output_grad = product('bokl,bekl->oe', spec_cot[:, :, 0], outward_real) - product('bokl,bekl->oe', spec_cot[:, :, 1], outward_imag)
    return (core_grad, input_grad, output_grad, height_grad, width_grad)
```

```python
import functools
import math

import jax
import jax.numpy as jnp
import numpy as np
from jax import lax
from jax.experimental import pallas as pl
from jax.experimental.pallas import tpu as pltpu
from jax.sharding import PartitionSpec as P

f32 = jnp.float32
bf16 = jnp.bfloat16
AXES = ("sp", "ch")
LANE = 128
VMEM_LIMIT = 60 * 1024 * 1024


def round_up(value, unit):
    return -(-value // unit) * unit


def row_tables(batch, width, modes):
    phases = (np.arange(width)[:, None] * np.arange(modes)[None, :] % width).astype(np.float32)
    angles = phases * np.float32(2.0 * math.pi / width)
    scaling = np.float32(1.0 / math.sqrt(width))
    table = np.concatenate([np.cos(angles) * scaling, -np.sin(angles) * scaling], axis=1)
    span = 2 * modes
    reach = max(round_up(b * span % LANE + span, LANE) for b in range(batch))
    full = np.zeros((batch, width, reach), np.float32)
    for b in range(batch):
        full[b, :, b * span % LANE : b * span % LANE + span] = table
    return jnp.asarray(full, dtype=bf16)


class Plan:
    def __init__(self, total, kept):
        bits = total.bit_length() - 1
        self.total = total
        self.halvings = 0
        while self.halvings < bits and kept % (2 << self.halvings) == 0:
            self.halvings += 1
        self.owners = 1 << self.halvings
        self.per = kept // self.owners
        first = list(range(self.halvings))
        second = list(first)
        if self.halvings > 2:
            second[1], second[2] = second[2], second[1]
        self.orders = (first, second)
        self.rest = list(range(self.halvings, bits))

    def flips(self, color):
        order = self.orders[color]
        masks = []
        for relative in range(self.owners):
            mask = 0
            for turn, bit in enumerate(order):
                if relative >> (self.halvings - 1 - turn) & 1:
                    mask |= 1 << bit
            masks.append(mask)
        return np.asarray(masks, dtype=np.int32)

    def swap(self, value, bit):
        pairs = [(i, i ^ (1 << bit)) for i in range(self.total)]
        return lax.ppermute(value, AXES, pairs)


def reduce_scatter(plan, color, keep, send):
    for turn, bit in enumerate(plan.orders[color]):
        total = keep + plan.swap(send, bit).astype(f32)
        if turn + 1 < plan.halvings:
            middle = total.shape[0] // 2
            keep, send = total[:middle], total[middle:].astype(bf16)
    for bit in plan.rest:
        value = total.astype(bf16)
        total = value.astype(f32) + plan.swap(value, bit).astype(f32)
    return total


def all_gather(plan, color, value):
    other = value
    for turn, bit in enumerate(reversed(plan.orders[color])):
        if turn > 0:
            value = jnp.concatenate([value, other], axis=0)
        other = plan.swap(value, bit)
    return value, other


def column_tables(plan, kept, rows_here, height, me, shard):
    owner = me & (plan.owners - 1)
    heights = shard * rows_here + jnp.arange(rows_here, dtype=jnp.int32)
    flips = jnp.asarray(np.stack([plan.flips(0), plan.flips(1)]))
    owned = jnp.bitwise_xor(owner, flips)
    ordinal = jnp.arange(plan.per, dtype=jnp.int32)[None, :, None] * plan.owners + owned[:, None, :]
    ordinal = ordinal.reshape(2, kept)
    frequency = jnp.where(ordinal < kept // 2, ordinal, ordinal + (height - kept))
    phases = (frequency[:, :, None] * heights[None, None, :] % height).astype(f32)
    angles = phases * (2.0 * math.pi / height)
    scaling = 1.0 / math.sqrt(height)
    cosine = (jnp.cos(angles) * scaling).astype(bf16)
    sines = (jnp.sin(angles) * scaling).astype(bf16)
    forth = jnp.concatenate([cosine, sines], axis=1)
    back = jnp.concatenate([jnp.swapaxes(cosine, 1, 2), jnp.swapaxes(sines, 1, 2)], axis=1)
    return forth, back


def turned(value, modes, sign):
    lanes = value.shape[1]
    lane = lax.broadcasted_iota(jnp.int32, value.shape, 1)
    even = (lane // modes) % 2 == 0
    ahead = pltpu.roll(value, lanes - modes, 1)
    behind = pltpu.roll(value, modes, 1)
    if sign > 0:
        return jnp.where(even, ahead, -behind)
    return jnp.where(even, -ahead, behind)


def forward_kernel(
    x_ref, table_ref, factor_ref, forth_ref, rows_ref, keep0_ref, send0_ref, keep1_ref, send1_ref,
    raw, projected, packed, *, plan, rank, rows_here,
):
    step = pl.program_id(0)
    batch, channels, block, width = x_ref.shape
    lanes = keep0_ref.shape[1]
    span = lanes // batch
    modes = span // 2
    tiles = lanes // LANE
    kept = plan.per * plan.owners
    half = rank // 2
    rank_pad = factor_ref.shape[0]
    segment = packed.shape[1] // (2 * plan.owners)
    reach = table_ref.shape[2] // LANE
    for b in range(batch):
        values = jnp.dot(x_ref[b].reshape(channels * block, width), table_ref[b], preferred_element_type=f32)
        for t in range(reach):
            raw[b * reach + t] = values[:, t * LANE : (t + 1) * LANE]
    for h in range(block):
        parts = [None] * tiles
        for b in range(batch):
            for t in range(reach):
                place = b * span // LANE + t
                if place < tiles:
                    piece = raw[b * reach + t, pl.ds(h, channels, stride=block), :]
                    parts[place] = piece if parts[place] is None else parts[place] + piece
        joined = jnp.concatenate(parts, axis=1).astype(bf16)
        rows_ref[:, h * lanes : (h + 1) * lanes] = joined
        mixed = jnp.dot(factor_ref[...], joined, preferred_element_type=f32)
        for t in range(tiles):
            projected[t, pl.ds(step * block + h, rank_pad, stride=rows_here), :] = mixed[:, t * LANE : (t + 1) * LANE]

    @pl.when(step == pl.num_programs(0) - 1)
    def _():
        if segment > plan.per * half:
            for color in range(2):
                for spare in range(plan.per * half, segment):
                    for t in range(tiles):
                        packed[t, pl.ds(color * plan.owners * segment + spare, plan.owners, stride=segment), :] = (
                            jnp.zeros((plan.owners, LANE), f32)
                        )
        for color in range(2):

            @pl.loop(0, half)
            def _(a):
                start = pl.multiple_of((color * half + a) * rows_here, 8)
                plane = jnp.concatenate(
                    [projected[t, pl.ds(start, rows_here), :] for t in range(tiles)], axis=1
                ).astype(bf16)
                both = jnp.dot(forth_ref[color], plane, preferred_element_type=f32)
                spectrum = both[:kept] + turned(both[kept:], modes, 1)
                for j in range(plan.per):
                    for t in range(tiles):
                        packed[
                            t, pl.ds(color * plan.owners * segment + j * half + a, plan.owners, stride=segment), :
                        ] = spectrum[j * plan.owners : (j + 1) * plan.owners, t * LANE : (t + 1) * LANE]

        middle = keep0_ref.shape[0]
        for t in range(tiles):
            for color, (keep_ref, send_ref) in enumerate(((keep0_ref, send0_ref), (keep1_ref, send1_ref))):
                start = 2 * color * middle
                keep_ref[:, t * LANE : (t + 1) * LANE] = packed[t, start : start + middle]
                send_ref[:, t * LANE : (t + 1) * LANE] = packed[t, start + middle : start + 2 * middle].astype(bf16)


def forward(plan, field, table, factor, forth, rank, modes):
    batch, channels, rows_here, width = field.shape
    span = 2 * modes
    lanes = batch * span
    kept = plan.per * plan.owners
    block = min(16, rows_here)
    segment = round_up(plan.per * rank // 2, 8)
    rank_pad = factor.shape[0]
    middle = plan.owners * segment // 2
    return pl.pallas_call(
        functools.partial(forward_kernel, plan=plan, rank=rank, rows_here=rows_here),
        grid=(rows_here // block,),
        in_specs=[
            pl.BlockSpec((batch, channels, block, width), lambda s: (0, 0, s, 0)),
            pl.BlockSpec(table.shape, lambda s: (0, 0, 0)),
            pl.BlockSpec((rank_pad, channels), lambda s: (0, 0)),
            pl.BlockSpec((2, 2 * kept, rows_here), lambda s: (0, 0, 0)),
        ],
        out_specs=[
            pl.BlockSpec((channels, block * lanes), lambda s: (0, s)),
        ]
        + [pl.BlockSpec((middle, lanes), lambda s: (0, 0))] * 4,
        out_shape=[
            jax.ShapeDtypeStruct((channels, rows_here * lanes), bf16),
        ]
        + [jax.ShapeDtypeStruct((middle, lanes), dtype) for dtype in (f32, bf16, f32, bf16)],
        scratch_shapes=[
            pltpu.VMEM((batch * table.shape[2] // LANE, channels * block, LANE), f32),
            pltpu.VMEM((lanes // LANE, rank_pad * rows_here, LANE), f32),
            pltpu.VMEM((lanes // LANE, 2 * plan.owners * segment, LANE), f32),
        ],
        compiler_params=pltpu.CompilerParams(vmem_limit_bytes=VMEM_LIMIT),
        cost_estimate=pl.CostEstimate(
            flops=2 * batch * channels * rows_here * width * span,
            bytes_accessed=2 * batch * channels * rows_here * (width + span),
            transcendentals=0,
        ),
    )(field, table, factor, forth)


def backward_kernel(
    g00_ref, g01_ref, g10_ref, g11_ref, rows_in_ref, rows_out_ref, back_ref, out_in_ref, out_out_ref,
    wide, grids_in, grids_out, block_in, block_out, *, plan, ranks, rows_here, modes,
):
    step = pl.program_id(0)
    tiles = wide.shape[0]
    lanes = tiles * LANE
    segments = [round_up(plan.per * rank // 2, 8) for rank in ranks]
    stride = sum(segments)

    @pl.when(step == 0)
    def _():
        out_in_ref[...] = jnp.zeros_like(out_in_ref)
        out_out_ref[...] = jnp.zeros_like(out_out_ref)
        for grids, rank in zip((grids_in, grids_out), ranks):
            spare = grids.shape[1] - rank * rows_here
            if spare:
                grids[:, rank * rows_here :, :] = jnp.zeros((tiles, spare, LANE), f32)
        for color, (one, other) in enumerate(((g00_ref, g01_ref), (g10_ref, g11_ref))):
            middle = one.shape[0]
            for t in range(tiles):
                wide[t, :middle, :] = one[:, t * LANE : (t + 1) * LANE].astype(f32)
                wide[t, middle:, :] = other[:, t * LANE : (t + 1) * LANE].astype(f32)
            for side, (grids, rank) in enumerate(zip((grids_in, grids_out), ranks)):
                half = rank // 2
                base = side * segments[0]

                @pl.loop(0, half)
                def _(a):
                    spectrum = jnp.concatenate(
                        [
                            jnp.concatenate(
                                [
                                    wide[t, pl.ds(base + j * half + a, plan.owners, stride=stride), :]
                                    for t in range(tiles)
                                ],
                                axis=1,
                            )
                            for j in range(plan.per)
                        ],
                        axis=0,
                    ).astype(bf16)
                    both = jnp.dot(back_ref[color], spectrum, preferred_element_type=f32)
                    start = pl.multiple_of((color * half + a) * rows_here, 8)
                    grid = both[:rows_here] + turned(both[rows_here:], modes, -1)
                    for t in range(tiles):
                        grids[t, pl.ds(start, rows_here), :] = grid[:, t * LANE : (t + 1) * LANE]

    for grids, block_ref, rows_ref, out_ref in (
        (grids_in, block_in, rows_in_ref, out_in_ref),
        (grids_out, block_out, rows_out_ref, out_out_ref),
    ):
        for h in range(block_ref.shape[1] // lanes):
            for t in range(tiles):
                block_ref[:, h * lanes + t * LANE : h * lanes + (t + 1) * LANE] = grids[
                    t, pl.ds(step * (block_ref.shape[1] // lanes) + h, block_ref.shape[0], stride=rows_here), :
                ].astype(bf16)
        out_ref[...] += lax.dot_general(
            rows_ref[...], block_ref[...], (((1,), (1,)), ((), ())), preferred_element_type=f32
        )


def backward(plan, pieces, rows_in, rows_out, back, ranks, rows_here, modes):
    channels = rows_in.shape[0]
    lanes = rows_in.shape[1] // rows_here
    block = min(16, rows_here)
    pads = [round_up(rank, 8) for rank in ranks]
    whole = lambda s: (0, 0)
    part = pl.BlockSpec((channels, block * lanes), lambda s: (0, s))
    return pl.pallas_call(
        functools.partial(backward_kernel, plan=plan, ranks=ranks, rows_here=rows_here, modes=modes),
        grid=(rows_here // block,),
        in_specs=[pl.BlockSpec(piece.shape, whole) for piece in pieces]
        + [part, part, pl.BlockSpec(back.shape, lambda s: (0, 0, 0))],
        out_specs=[pl.BlockSpec((channels, pad), whole) for pad in pads],
        out_shape=[jax.ShapeDtypeStruct((channels, pad), f32) for pad in pads],
        scratch_shapes=[pltpu.VMEM((lanes // LANE, 2 * pieces[0].shape[0], LANE), f32)]
        + [pltpu.VMEM((lanes // LANE, pad * rows_here, LANE), f32) for pad in pads]
        + [pltpu.VMEM((pad, block * lanes), bf16) for pad in pads],
        compiler_params=pltpu.CompilerParams(vmem_limit_bytes=VMEM_LIMIT),
        cost_estimate=pl.CostEstimate(
            flops=2 * channels * sum(pads) * rows_here * lanes,
            bytes_accessed=4 * channels * rows_here * lanes,
            transcendentals=0,
        ),
    )(*pieces, rows_in, rows_out, back)


def owner_kernel(
    left0_ref, left1_ref, right0_ref, right1_ref, core_ref, core_t_ref, modes_ref, height_ref, width_ref,
    core_out, height_out, width_out, back0_ref, back1_ref, modal, pair, pair_low,
    *, plan, batch, rank_in, rank_out, modes,
):
    pad_in, pad_out = round_up(rank_in, 8), round_up(rank_out, 8)
    lanes = left0_ref.shape[1]
    plane = modes_ref.shape[2]
    segment_in = left0_ref.shape[0]
    rows = rank_in * pad_out

    def gathered(refs, j, rank, pad):
        half = rank // 2
        parts = [ref[...].astype(f32)[j * half : (j + 1) * half] for ref in refs]
        if pad > rank:
            parts.append(jnp.zeros((pad - rank, lanes), f32))
        joined = jnp.concatenate(parts, axis=0)
        pieces = []
        for n in range(2 * batch):
            turned_by = (lanes - n * modes) % lanes
            piece = pltpu.roll(joined, turned_by, 1) if turned_by else joined
            pieces.append(piece[:, :plane])
        return pieces

    lane = lax.broadcasted_iota(jnp.int32, (1, plane), 1) < modes

    def spread(pieces):
        total = None
        for n, piece in enumerate(pieces):
            kept = jnp.where(lane, piece, 0.0)
            wide = jnp.concatenate([kept, jnp.zeros((kept.shape[0], lanes - plane), f32)], axis=1)
            wide = pltpu.roll(wide, n * modes, 1) if n else wide
            total = wide if total is None else total + wide
        return total

    core_sum = None
    width_sum = None
    for j in range(plan.per):
        left = gathered((left0_ref, left1_ref), j, rank_in, pad_in)
        right = gathered((right0_ref, right1_ref), j, rank_out, pad_out)
        table = modes_ref[j].astype(bf16)
        table_low = (modes_ref[j] - table.astype(f32)).astype(bf16)
        modal[...] = (
            jnp.dot(core_ref[0], table, preferred_element_type=f32)
            + jnp.dot(core_ref[1], table, preferred_element_type=f32)
            + jnp.dot(core_ref[0], table_low, preferred_element_type=f32)
        )
        inward = [[] for _ in range(2 * batch)]
        outward = [jnp.zeros((pad_out, plane), f32) for _ in range(2 * batch)]
        for a in range(rank_in):
            modal_real = modal[a * pad_out : (a + 1) * pad_out]
            modal_imag = modal[rows + a * pad_out : rows + (a + 1) * pad_out]
            pair_real = jnp.zeros((pad_out, plane), f32)
            pair_imag = jnp.zeros((pad_out, plane), f32)
            for b in range(batch):
                left_real = left[2 * b][a : a + 1]
                left_imag = -left[2 * b + 1][a : a + 1]
                right_real = right[2 * b]
                right_imag = right[2 * b + 1]
                pair_real += left_real * right_real - left_imag * right_imag
                pair_imag += left_real * right_imag + left_imag * right_real
                inward[2 * b].append(
                    jnp.sum(modal_real * right_real + modal_imag * right_imag, axis=0, keepdims=True)
                )
                inward[2 * b + 1].append(
                    jnp.sum(modal_real * right_imag - modal_imag * right_real, axis=0, keepdims=True)
                )
                outward[2 * b] += modal_real * left_real + modal_imag * left_imag
                outward[2 * b + 1] -= modal_real * left_imag - modal_imag * left_real
            for start, value in ((a * pad_out, pair_real), (rows + a * pad_out, pair_imag)):
                high = value.astype(bf16)
                pair[start : start + pad_out] = high
                pair_low[start : start + pad_out] = (value - high.astype(f32)).astype(bf16)
        contract = (((1,), (1,)), ((), ()))
        part = (
            lax.dot_general(pair[...], table, contract, preferred_element_type=f32)
            + lax.dot_general(pair_low[...], table, contract, preferred_element_type=f32)
            + lax.dot_general(pair[...], table_low, contract, preferred_element_type=f32)
        )
        core_sum = part if j == 0 else core_out[...] + part
        core_out[...] = core_sum
        terms = (
            jnp.dot(core_t_ref[0], pair[...], preferred_element_type=f32)
            + jnp.dot(core_t_ref[1], pair[...], preferred_element_type=f32)
            + jnp.dot(core_t_ref[0], pair_low[...], preferred_element_type=f32)
        )
        height_out[j] = jnp.sum(terms * width_ref[...], axis=1, keepdims=True)
        by_width = terms * height_ref[j]
        width_sum = by_width if j == 0 else width_sum + by_width
        half_in, half_out = rank_in // 2, rank_out // 2
        inward_all = spread([jnp.concatenate(rows_of, axis=0) for rows_of in inward])
        outward_all = spread(outward)
        for color, ref in enumerate((back0_ref, back1_ref)):
            ref[j * half_in : (j + 1) * half_in] = inward_all[color * half_in : (color + 1) * half_in]
            ref[segment_in + j * half_out : segment_in + (j + 1) * half_out] = outward_all[
                color * half_out : (color + 1) * half_out
            ]
    for ref in (back0_ref, back1_ref):
        for start, used, stop in (
            (0, plan.per * rank_in // 2, segment_in),
            (segment_in, plan.per * rank_out // 2, ref.shape[0]),
        ):
            if start + used < stop:
                ref[start + used : stop] = jnp.zeros((stop - start - used, lanes), f32)
    width_out[...] = width_sum


def owner_work(plan, left, right, core_tensor, height_rows, width_factor, batch):
    _, rank_in, rank_out, rank_x, rank_y = core_tensor.shape
    modes = width_factor.shape[0]
    pad_out = round_up(rank_out, 8)
    pairs = round_up(rank_x * rank_y, 8)
    plane = round_up(modes, 128)
    lanes = left[0].shape[1]
    rows = left[0].shape[0] + right[0].shape[0]
    spare = pairs - rank_x * rank_y
    core = core_tensor.reshape(2, rank_in, rank_out, rank_x * rank_y)
    core = jnp.pad(core, ((0, 0), (0, 0), (0, pad_out - rank_out), (0, spare)))
    core = core.reshape(2 * rank_in * pad_out, pairs)
    core_high = core.astype(bf16)
    core = jnp.stack([core_high, (core - core_high.astype(f32)).astype(bf16)])
    width_turned = jnp.pad(width_factor.T, ((0, 0), (0, plane - modes)))
    width_wide = jnp.broadcast_to(width_turned[None], (rank_x, rank_y, plane)).reshape(rank_x * rank_y, plane)
    width_wide = jnp.pad(width_wide, ((0, spare), (0, 0)))
    height_wide = jnp.broadcast_to(height_rows[:, :, None], (plan.per, rank_x, rank_y))
    height_wide = jnp.pad(height_wide.reshape(plan.per, rank_x * rank_y, 1), ((0, 0), (0, spare), (0, 0)))
    table = height_wide * width_wide[None]
    core_part, height_part, width_part, back0, back1 = pl.pallas_call(
        functools.partial(
            owner_kernel, plan=plan, batch=batch, rank_in=rank_in, rank_out=rank_out, modes=modes
        ),
        out_shape=[
            jax.ShapeDtypeStruct((2 * rank_in * pad_out, pairs), f32),
            jax.ShapeDtypeStruct((plan.per, pairs, 1), f32),
            jax.ShapeDtypeStruct((pairs, plane), f32),
            jax.ShapeDtypeStruct((rows, lanes), f32),
            jax.ShapeDtypeStruct((rows, lanes), f32),
        ],
        scratch_shapes=[
            pltpu.VMEM((2 * rank_in * pad_out, plane), f32),
            pltpu.VMEM((2 * rank_in * pad_out, plane), bf16),
            pltpu.VMEM((2 * rank_in * pad_out, plane), bf16),
        ],
        compiler_params=pltpu.CompilerParams(vmem_limit_bytes=VMEM_LIMIT),
    )(*left, *right, core, jnp.swapaxes(core, 1, 2), table, height_wide, width_wide)
    height_part = height_part[:, : rank_x * rank_y, 0].reshape(plan.per, rank_x, rank_y).sum(axis=2)
    width_part = width_part[: rank_x * rank_y, :modes].reshape(rank_x, rank_y, modes).sum(axis=0)
    return core_part, height_part, width_part, (back0.astype(bf16), back1.astype(bf16))


def all_reduce(plan, bits, value):
    for bit in bits:
        value = value + plan.swap(value, bit)
    return value


def all_reduce_large(plan, me, value):
    split = []
    for bit in range(plan.total.bit_length() - 1):
        if value.shape[0] % 16 == 0 and len(split) < 3:
            middle = value.shape[0] // 2
            high = (me >> bit) & 1
            keep = lax.dynamic_slice_in_dim(value, high * middle, middle, 0)
            send = lax.dynamic_slice_in_dim(value, (1 - high) * middle, middle, 0).astype(bf16)
            value = keep + plan.swap(send, bit).astype(f32)
            split.append((bit, high))
        else:
            sent = value.astype(bf16)
            value = sent.astype(f32) + plan.swap(sent, bit).astype(f32)
    value = value.astype(bf16)
    for bit, high in reversed(split):
        other = plan.swap(value, bit)
        value = jnp.where(
            high == 0, jnp.concatenate([value, other], axis=0), jnp.concatenate([other, value], axis=0)
        )
    return value.astype(f32)


def on_device(inputs, cotangent, input_factor, output_factor, height_factor, width_factor, core_tensor):
    batch, channels, rows_here, width = inputs.shape
    kept, rank_x = height_factor.shape
    modes, rank_y = width_factor.shape
    rank_in, rank_out = input_factor.shape[1], output_factor.shape[1]
    shards, blocks = lax.axis_size("sp"), lax.axis_size("ch")
    shard = lax.axis_index("sp")
    me = shard * blocks + lax.axis_index("ch")
    plan = Plan(shards * blocks, kept)
    table = row_tables(batch, width, modes)
    forth, back = column_tables(plan, kept, rows_here, rows_here * shards, me, shard)

    def padded(factor):
        rank = factor.shape[1]
        return jnp.pad(factor.T, ((0, round_up(rank, 8) - rank), (0, 0)))

    def scattered(parts):
        return [reduce_scatter(plan, color, parts[2 * color], parts[2 * color + 1]) for color in range(2)]

    rows_input, *left = forward(plan, inputs, table, padded(input_factor), forth, rank_in, modes)
    left = scattered(left)
    rows_cot, *right = forward(plan, cotangent, table, padded(output_factor), forth, rank_out, modes)
    right = scattered(right)

    owner = me & (plan.owners - 1)
    height_rows = height_factor[jnp.arange(plan.per) * plan.owners + owner]
    core_part, height_part, width_part, back_parts = owner_work(
        plan, left, right, core_tensor, height_rows, width_factor, batch
    )
    pieces = []
    for color in range(2):
        pieces.extend(all_gather(plan, color, back_parts[color]))

    counts = (me >> plan.halvings) == 0
    height_full = jnp.zeros((plan.per, plan.owners, rank_x), f32)
    height_full = lax.dynamic_update_slice(height_full, height_part[:, None], (0, owner, 0)).reshape(kept, rank_x)
    small = jnp.concatenate([height_full.T, width_part], axis=0)
    core_rows, core_lanes = core_part.shape
    total_rows = round_up(core_rows + small.shape[0], 64)
    wide_lanes = max(core_lanes, small.shape[1])
    summed = jnp.concatenate(
        [
            jnp.pad(core_part, ((0, 0), (0, wide_lanes - core_lanes))),
            jnp.pad(small, ((0, total_rows - core_rows - small.shape[0]), (0, wide_lanes - small.shape[1]))),
        ],
        axis=0,
    )
    summed = all_reduce_large(plan, me, jnp.where(counts, summed, 0.0))
    core_grad = summed[:core_rows].reshape(2, rank_in, -1, wide_lanes)[:, :, :rank_out, : rank_x * rank_y]
    core_grad = core_grad.reshape(core_tensor.shape)
    height_grad = summed[core_rows : core_rows + rank_x, :kept].T
    width_grad = summed[core_rows + rank_x : core_rows + rank_x + rank_y, :modes].T

    input_part, output_part = backward(
        plan, pieces, rows_input, rows_cot, back, (rank_in, rank_out), rows_here, modes
    )
    input_part, output_part = input_part[:, :rank_in], output_part[:, :rank_out]
    over_rows = range(blocks.bit_length() - 1, plan.total.bit_length() - 1)
    both = all_reduce(plan, over_rows, jnp.concatenate([input_part, output_part], axis=0))
    return (core_grad, both[:channels], both[channels:], height_grad, width_grad)


def solution(mesh):
    placed = (
        P(None, "ch", "sp", None),
        P(None, "ch", "sp", None),
        P("ch", None),
        P("ch", None),
        P(),
        P(),
        P(),
    )
    return jax.shard_map(
        on_device,
        mesh=mesh,
        in_specs=placed,
        out_specs=(P(), P("ch", None), P("ch", None), P(), P()),
        check_vma=False,
    )
```

```python
import functools
import math

import jax
import jax.numpy as jnp
import numpy as np
from jax import lax
from jax.experimental import pallas as pl
from jax.experimental.pallas import tpu as pltpu
from jax.sharding import PartitionSpec as P

f32 = jnp.float32
bf16 = jnp.bfloat16
AXES = ("sp", "ch")
LANE = 128
VMEM_LIMIT = 60 * 1024 * 1024


def round_up(value, unit):
    return -(-value // unit) * unit


def row_tables(batch, width, modes):
    phases = (np.arange(width)[:, None] * np.arange(modes)[None, :] % width).astype(np.float32)
    angles = phases * np.float32(2.0 * math.pi / width)
    scaling = np.float32(1.0 / math.sqrt(width))
    table = np.concatenate([np.cos(angles) * scaling, -np.sin(angles) * scaling], axis=1)
    base = jnp.asarray(table, dtype=bf16)
    span = 2 * modes
    reach = max(round_up(b * span % LANE + span, LANE) for b in range(batch))
    starts = [b * span % LANE for b in range(batch)]
    return jnp.stack([jnp.pad(base, ((0, 0), (start, reach - start - span))) for start in starts])


class Plan:
    def __init__(self, total, kept):
        bits = total.bit_length() - 1
        self.total = total
        self.halvings = 0
        while self.halvings < bits and kept % (2 << self.halvings) == 0:
            self.halvings += 1
        self.owners = 1 << self.halvings
        self.per = kept // self.owners
        first = list(range(self.halvings))
        second = list(first)
        if self.halvings > 2:
            second[1], second[2] = second[2], second[1]
        self.orders = (first, second)
        self.rest = list(range(self.halvings, bits))
        self.turns = [[turn] for turn in range(self.halvings)]

    def flips(self, color):
        order = self.orders[color]
        masks = []
        for relative in range(self.owners):
            mask = 0
            for turn, bit in enumerate(order):
                if relative >> (self.halvings - 1 - turn) & 1:
                    mask |= 1 << bit
            masks.append(mask)
        return np.asarray(masks, dtype=np.int32)

    def masks(self, color, turn):
        bits = [self.orders[color][t] for t in self.turns[turn]]
        return [
            sum(1 << bit for place, bit in enumerate(bits) if part >> (len(bits) - 1 - place) & 1)
            for part in range(1, 1 << len(bits))
        ]

    def trade(self, value, mask):
        return lax.ppermute(value, AXES, [(i, i ^ mask) for i in range(self.total)])

    def swap(self, value, bit):
        return self.trade(value, 1 << bit)


def first_exchange(plan, keep, send):
    if plan.halvings == 0:
        return keep
    return keep + plan.swap(send, plan.orders[0][0]).astype(f32)


def reduce_scatter(plan, fields, late):
    keeps = [jnp.stack([field[color] for field in fields]) for color in range(2)]
    arrived = []
    for turn in range(1, len(plan.turns)):
        keeps = [sum([other[color].astype(f32) for other in arrived], keeps[color]) for color in range(2)]
        if turn == 2:
            keeps, late = lax.optimization_barrier((keeps, late))
        parts = 1 << len(plan.turns[turn])
        size = keeps[0].shape[1] // parts
        masks = [plan.masks(color, turn) for color in range(2)]
        arrived = []
        for part in range(1, parts):
            sends = [keep[:, part * size : (part + 1) * size].astype(bf16) for keep in keeps]
            if masks[0] == masks[1]:
                arrived.append(plan.trade(jnp.stack(sends), masks[0][part - 1]))
            else:
                arrived.append([plan.trade(sends[color], masks[color][part - 1]) for color in range(2)])
        keeps = [keep[:, :size] for keep in keeps]
    keep = jnp.stack(keeps)
    arrived = [other if isinstance(other, jax.Array) else jnp.stack(other) for other in arrived]
    for bit in plan.rest:
        value = sum([other.astype(f32) for other in arrived], keep).astype(bf16)
        keep, arrived = value.astype(f32), [plan.swap(value, bit)]
    return keep, arrived, late


def all_gather(plan, both):
    values = None
    for turn in reversed(range(len(plan.turns))):
        masks = [plan.masks(color, turn) for color in range(2)]
        if values is None:
            if masks[0] == masks[1]:
                others = [plan.trade(both, mask) for mask in masks[0]]
            else:
                others = list(zip(*[[plan.trade(both[color], mask) for mask in masks[color]] for color in range(2)]))
            values = [both[0], both[1]]
        else:
            values = [jnp.concatenate([values[color]] + [o[color] for o in others], axis=0) for color in range(2)]
            if masks[0] == masks[1] and turn > 0:
                both = jnp.stack(values)
                others = [plan.trade(both, mask) for mask in masks[0]]
                continue
            others = list(zip(*[[plan.trade(values[color], mask) for mask in masks[color]] for color in range(2)]))
    return [values[0], others[0][0], values[1], others[0][1]]


def column_tables(plan, kept, rows_here, height, me, shard):
    owner = me & (plan.owners - 1)
    heights = shard * rows_here + jnp.arange(rows_here, dtype=jnp.int32)
    flips = jnp.asarray(np.stack([plan.flips(0), plan.flips(1)]))
    owned = jnp.bitwise_xor(owner, flips)
    ordinal = jnp.arange(plan.per, dtype=jnp.int32)[None, :, None] * plan.owners + owned[:, None, :]
    ordinal = ordinal.reshape(2, kept)
    frequency = jnp.where(ordinal < kept // 2, ordinal, ordinal + (height - kept))
    phases = (frequency[:, :, None] * heights[None, None, :] % height).astype(f32)
    angles = phases * (2.0 * math.pi / height)
    scaling = 1.0 / math.sqrt(height)
    cosine = (jnp.cos(angles) * scaling).astype(bf16)
    sines = (jnp.sin(angles) * scaling).astype(bf16)
    forth = jnp.concatenate([cosine, sines], axis=1)
    back = jnp.concatenate([jnp.swapaxes(cosine, 1, 2), jnp.swapaxes(sines, 1, 2)], axis=1)
    return forth, back


def turned(value, modes, sign):
    lanes = value.shape[1]
    lane = lax.broadcasted_iota(jnp.int32, value.shape, 1)
    even = (lane // modes) % 2 == 0
    ahead = pltpu.roll(value, lanes - modes, 1)
    behind = pltpu.roll(value, modes, 1)
    if sign > 0:
        return jnp.where(even, ahead, -behind)
    return jnp.where(even, -ahead, behind)


def forward_kernel(
    x_ref, table_ref, factor_ref, forth_ref, rows_ref, keep_ref, send_ref,
    raw, projected, packed, *, plan, rank, rows_here,
):
    step = pl.program_id(0)
    batch, channels, block, width = x_ref.shape
    lanes = keep_ref.shape[1]
    span = lanes // batch
    modes = span // 2
    tiles = lanes // LANE
    kept = plan.per * plan.owners
    half = rank // 2
    rank_pad = factor_ref.shape[0]
    segment = packed.shape[1] // (2 * plan.owners)
    reach = table_ref.shape[2] // LANE
    gap = block + 8
    some = max(1, 256 // block)
    for b in range(batch):
        for first in range(0, channels, some):
            values = jnp.dot(
                x_ref[b, first : first + some].reshape(some * block, width), table_ref[b], preferred_element_type=f32
            )
            for t in range(reach):
                for i in range(some):
                    raw[b * reach + t, (first + i) * gap : (first + i) * gap + block] = values[
                        i * block : (i + 1) * block, t * LANE : (t + 1) * LANE
                    ]
    for h in range(block):
        parts = [None] * tiles
        for b in range(batch):
            for t in range(reach):
                place = b * span // LANE + t
                if place < tiles:
                    piece = raw[b * reach + t, pl.ds(h, channels, stride=gap), :]
                    parts[place] = piece if parts[place] is None else parts[place] + piece
        joined = jnp.concatenate(parts, axis=1).astype(bf16)
        rows_ref[:, h * lanes : (h + 1) * lanes] = joined
        mixed = jnp.dot(factor_ref[...], joined, preferred_element_type=f32)
        for t in range(tiles):
            projected[t, pl.ds(step * block + h, rank_pad, stride=rows_here + 8), :] = mixed[:, t * LANE : (t + 1) * LANE]

    @pl.when(step == pl.num_programs(0) - 1)
    def _():
        if segment > plan.per * half:
            for color in range(2):
                for spare in range(plan.per * half, segment):
                    for t in range(tiles):
                        packed[t, pl.ds(color * plan.owners * segment + spare, plan.owners, stride=segment), :] = (
                            jnp.zeros((plan.owners, LANE), f32)
                        )
        for color in range(2):

            @pl.loop(0, half, unroll=True)
            def _(a):
                start = pl.multiple_of((color * half + a) * (rows_here + 8), 8)
                plane = jnp.concatenate(
                    [projected[t, pl.ds(start, rows_here), :] for t in range(tiles)], axis=1
                ).astype(bf16)
                both = jnp.dot(forth_ref[color], plane, preferred_element_type=f32)
                spectrum = both[:kept] + turned(both[kept:], modes, 1)
                for j in range(plan.per):
                    for t in range(tiles):
                        packed[
                            t, pl.ds(color * plan.owners * segment + j * half + a, plan.owners, stride=segment), :
                        ] = spectrum[j * plan.owners : (j + 1) * plan.owners, t * LANE : (t + 1) * LANE]

        middle = keep_ref.shape[0] // 2
        for t in range(tiles):
            for color in range(2):
                here, start = slice(color * middle, (color + 1) * middle), 2 * color * middle
                keep_ref[here, t * LANE : (t + 1) * LANE] = packed[t, start : start + middle]
                send_ref[here, t * LANE : (t + 1) * LANE] = packed[t, start + middle : start + 2 * middle].astype(bf16)


def forward(plan, field, table, factor, forth, rank, modes):
    batch, channels, rows_here, width = field.shape
    span = 2 * modes
    lanes = batch * span
    kept = plan.per * plan.owners
    block = min(16, rows_here)
    segment = round_up(plan.per * rank // 2, 8)
    rank_pad = factor.shape[0]
    middle = plan.owners * segment // 2
    return pl.pallas_call(
        functools.partial(forward_kernel, plan=plan, rank=rank, rows_here=rows_here),
        grid=(rows_here // block,),
        in_specs=[
            pl.BlockSpec((batch, channels, block, width), lambda s: (0, 0, s, 0)),
            pl.BlockSpec(table.shape, lambda s: (0, 0, 0)),
            pl.BlockSpec((rank_pad, channels), lambda s: (0, 0)),
            pl.BlockSpec((2, 2 * kept, rows_here), lambda s: (0, 0, 0)),
        ],
        out_specs=[
            pl.BlockSpec((channels, block * lanes), lambda s: (0, s)),
        ]
        + [pl.BlockSpec((2 * middle, lanes), lambda s: (0, 0))] * 2,
        out_shape=[
            jax.ShapeDtypeStruct((channels, rows_here * lanes), bf16),
        ]
        + [jax.ShapeDtypeStruct((2 * middle, lanes), dtype) for dtype in (f32, bf16)],
        scratch_shapes=[
            pltpu.VMEM((batch * table.shape[2] // LANE, channels * (block + 8), LANE), f32),
            pltpu.VMEM((lanes // LANE, rank_pad * (rows_here + 8), LANE), f32),
            pltpu.VMEM((lanes // LANE, 2 * plan.owners * segment, LANE), f32),
        ],
        compiler_params=pltpu.CompilerParams(vmem_limit_bytes=VMEM_LIMIT),
        cost_estimate=pl.CostEstimate(
            flops=2 * batch * channels * rows_here * width * span,
            bytes_accessed=2 * batch * channels * rows_here * (width + span),
            transcendentals=0,
        ),
    )(field, table, factor, forth)


def backward_kernel(
    g00_ref, g01_ref, g10_ref, g11_ref, rows_in_ref, rows_out_ref, back_ref, out_ref,
    wide, grids_in, grids_out, block_in, block_out, *, plan, ranks, rows_here, modes,
):
    step = pl.program_id(0)
    tiles = wide.shape[0]
    lanes = tiles * LANE
    segments = [round_up(plan.per * rank // 2, 8) for rank in ranks]
    used = sum(segments)
    stride = used + (8 if used // 8 % 2 == 0 else 16)
    channels = rows_in_ref.shape[0]

    @pl.when(step == 0)
    def _():
        out_ref[...] = jnp.zeros_like(out_ref)
        for grids, rank in zip((grids_in, grids_out), ranks):
            spare = grids.shape[1] - rank * (rows_here + 8)
            if spare:
                grids[:, rank * (rows_here + 8) :, :] = jnp.zeros((tiles, spare, LANE), f32)
        for color, (one, other) in enumerate(((g00_ref, g01_ref), (g10_ref, g11_ref))):
            for t in range(tiles):
                for relative in range(plan.owners):
                    piece = one if relative < plan.owners // 2 else other
                    start = relative % (plan.owners // 2) * used
                    wide[t, relative * stride : relative * stride + used, :] = piece[
                        start : start + used, t * LANE : (t + 1) * LANE
                    ].astype(f32)
            for side, (grids, rank) in enumerate(zip((grids_in, grids_out), ranks)):
                half = rank // 2
                base = side * segments[0]

                @pl.loop(0, half, unroll=True)
                def _(a):
                    spectrum = jnp.concatenate(
                        [
                            jnp.concatenate(
                                [
                                    wide[t, pl.ds(base + j * half + a, plan.owners, stride=stride), :]
                                    for t in range(tiles)
                                ],
                                axis=1,
                            )
                            for j in range(plan.per)
                        ],
                        axis=0,
                    ).astype(bf16)
                    both = jnp.dot(back_ref[color], spectrum, preferred_element_type=f32)
                    start = pl.multiple_of((color * half + a) * (rows_here + 8), 8)
                    grid = both[:rows_here] + turned(both[rows_here:], modes, -1)
                    for t in range(tiles):
                        grids[t, pl.ds(start, rows_here), :] = grid[:, t * LANE : (t + 1) * LANE]

    for side, (grids, block_ref, rows_ref) in enumerate(
        ((grids_in, block_in, rows_in_ref), (grids_out, block_out, rows_out_ref))
    ):
        for h in range(block_ref.shape[1] // lanes):
            for t in range(tiles):
                block_ref[:, h * lanes + t * LANE : h * lanes + (t + 1) * LANE] = grids[
                    t, pl.ds(step * (block_ref.shape[1] // lanes) + h, block_ref.shape[0], stride=rows_here + 8), :
                ].astype(bf16)
        out_ref[side * channels : (side + 1) * channels, : block_ref.shape[0]] += lax.dot_general(
            rows_ref[...], block_ref[...], (((1,), (1,)), ((), ())), preferred_element_type=f32
        )


def backward(plan, pieces, rows_in, rows_out, back, ranks, rows_here, modes):
    channels = rows_in.shape[0]
    lanes = rows_in.shape[1] // rows_here
    block = min(16, rows_here)
    pads = [round_up(rank, 8) for rank in ranks]
    whole = lambda s: (0, 0)
    part = pl.BlockSpec((channels, block * lanes), lambda s: (0, s))
    return pl.pallas_call(
        functools.partial(backward_kernel, plan=plan, ranks=ranks, rows_here=rows_here, modes=modes),
        grid=(rows_here // block,),
        in_specs=[pl.BlockSpec(piece.shape, whole) for piece in pieces]
        + [part, part, pl.BlockSpec(back.shape, lambda s: (0, 0, 0))],
        out_specs=pl.BlockSpec((2 * channels, max(pads)), whole),
        out_shape=jax.ShapeDtypeStruct((2 * channels, max(pads)), f32),
        scratch_shapes=[pltpu.VMEM((lanes // LANE, 2 * pieces[0].shape[0] + 16 * plan.owners, LANE), f32)]
        + [pltpu.VMEM((lanes // LANE, pad * (rows_here + 8), LANE), f32) for pad in pads]
        + [pltpu.VMEM((pad, block * lanes), bf16) for pad in pads],
        compiler_params=pltpu.CompilerParams(vmem_limit_bytes=VMEM_LIMIT),
        cost_estimate=pl.CostEstimate(
            flops=2 * channels * sum(pads) * rows_here * lanes,
            bytes_accessed=4 * channels * rows_here * lanes,
            transcendentals=0,
        ),
    )(*pieces, rows_in, rows_out, back)


def owner_kernel(
    keep_ref, core_ref, core_t_ref, modes_ref, height_ref, width_ref, *refs, plan, batch, rank_in, rank_out, modes,
):
    pad_in, pad_out = round_up(rank_in, 8), round_up(rank_out, 8)
    lanes = keep_ref.shape[3]
    plane = modes_ref.shape[2]
    segment_in = keep_ref.shape[2]
    *arrived, core_out, height_out, width_out, back_ref, modal, pair, pair_low, returned = refs
    sums = [sum([ref[:, side].astype(f32) for ref in arrived], keep_ref[:, side]) for side in range(2)]
    rows = rank_in * pad_out

    def gathered(sums, j, rank, pad):
        half = rank // 2
        parts = [sums[color, j * half : (j + 1) * half] for color in range(2)]
        if pad > rank:
            parts.append(jnp.zeros((pad - rank, lanes), f32))
        joined = jnp.concatenate(parts, axis=0)
        pieces = []
        for n in range(2 * batch):
            turned_by = (lanes - n * modes) % lanes
            piece = pltpu.roll(joined, turned_by, 1) if turned_by else joined
            pieces.append(piece[:, :plane])
        return pieces

    lane = lax.broadcasted_iota(jnp.int32, (1, plane), 1) < modes

    def spread(pieces):
        total = None
        for n, piece in enumerate(pieces):
            kept = jnp.where(lane, piece, 0.0)
            wide = jnp.concatenate([kept, jnp.zeros((kept.shape[0], lanes - plane), f32)], axis=1)
            wide = pltpu.roll(wide, n * modes, 1) if n else wide
            total = wide if total is None else total + wide
        return total

    core_sum = None
    width_sum = None
    for j in range(plan.per):
        left = gathered(sums[0], j, rank_in, pad_in)
        right = gathered(sums[1], j, rank_out, pad_out)
        table = modes_ref[j].astype(bf16)
        table_low = (modes_ref[j] - table.astype(f32)).astype(bf16)
        modal[...] = (
            jnp.dot(core_ref[0], table, preferred_element_type=f32)
            + jnp.dot(core_ref[1], table, preferred_element_type=f32)
            + jnp.dot(core_ref[0], table_low, preferred_element_type=f32)
        )
        inward = [[] for _ in range(2 * batch)]
        outward = [jnp.zeros((pad_out, plane), f32) for _ in range(2 * batch)]
        for a in range(rank_in):
            modal_real = modal[a * pad_out : (a + 1) * pad_out]
            modal_imag = modal[rows + a * pad_out : rows + (a + 1) * pad_out]
            pair_real = jnp.zeros((pad_out, plane), f32)
            pair_imag = jnp.zeros((pad_out, plane), f32)
            for b in range(batch):
                left_real = left[2 * b][a : a + 1]
                left_imag = -left[2 * b + 1][a : a + 1]
                right_real = right[2 * b]
                right_imag = right[2 * b + 1]
                pair_real += left_real * right_real - left_imag * right_imag
                pair_imag += left_real * right_imag + left_imag * right_real
                inward[2 * b].append(
                    jnp.sum(modal_real * right_real + modal_imag * right_imag, axis=0, keepdims=True)
                )
                inward[2 * b + 1].append(
                    jnp.sum(modal_real * right_imag - modal_imag * right_real, axis=0, keepdims=True)
                )
                outward[2 * b] += modal_real * left_real + modal_imag * left_imag
                outward[2 * b + 1] -= modal_real * left_imag - modal_imag * left_real
            for start, value in ((a * pad_out, pair_real), (rows + a * pad_out, pair_imag)):
                high = value.astype(bf16)
                pair[start : start + pad_out] = high
                pair_low[start : start + pad_out] = (value - high.astype(f32)).astype(bf16)
        contract = (((1,), (1,)), ((), ()))
        part = (
            lax.dot_general(pair[...], table, contract, preferred_element_type=f32)
            + lax.dot_general(pair_low[...], table, contract, preferred_element_type=f32)
            + lax.dot_general(pair[...], table_low, contract, preferred_element_type=f32)
        )
        core_sum = part if j == 0 else core_out[...] + part
        core_out[...] = core_sum
        terms = (
            jnp.dot(core_t_ref[0], pair[...], preferred_element_type=f32)
            + jnp.dot(core_t_ref[1], pair[...], preferred_element_type=f32)
            + jnp.dot(core_t_ref[0], pair_low[...], preferred_element_type=f32)
        )
        height_out[j] = jnp.sum(terms * width_ref[...], axis=1, keepdims=True)
        by_width = terms * height_ref[j]
        width_sum = by_width if j == 0 else width_sum + by_width
        half_in, half_out = rank_in // 2, rank_out // 2
        inward_all = spread([jnp.concatenate(rows_of, axis=0) for rows_of in inward])
        outward_all = spread(outward)
        for color in range(2):
            returned[color, j * half_in : (j + 1) * half_in] = inward_all[color * half_in : (color + 1) * half_in]
            returned[color, segment_in + j * half_out : segment_in + (j + 1) * half_out] = outward_all[
                color * half_out : (color + 1) * half_out
            ]
    for color in range(2):
        for start, used, stop in (
            (0, plan.per * rank_in // 2, segment_in),
            (segment_in, plan.per * rank_out // 2, returned.shape[1]),
        ):
            if start + used < stop:
                returned[color, start + used : stop] = jnp.zeros((stop - start - used, lanes), f32)
    back_ref[...] = returned[...].astype(bf16)
    width_out[...] = width_sum


def owner_work(plan, keep, arrived, core_tensor, height_rows, width_factor, batch):
    _, rank_in, rank_out, rank_x, rank_y = core_tensor.shape
    modes = width_factor.shape[0]
    pad_out = round_up(rank_out, 8)
    pairs = round_up(rank_x * rank_y, 8)
    plane = round_up(modes, 128)
    lanes = keep.shape[3]
    rows = 2 * keep.shape[2]
    spare = pairs - rank_x * rank_y
    core = core_tensor.reshape(2, rank_in, rank_out, rank_x * rank_y)
    core = jnp.pad(core, ((0, 0), (0, 0), (0, pad_out - rank_out), (0, spare)))
    core = core.reshape(2 * rank_in * pad_out, pairs)
    core_high = core.astype(bf16)
    core = jnp.stack([core_high, (core - core_high.astype(f32)).astype(bf16)])
    width_turned = jnp.pad(width_factor.T, ((0, 0), (0, plane - modes)))
    width_wide = jnp.broadcast_to(width_turned[None], (rank_x, rank_y, plane)).reshape(rank_x * rank_y, plane)
    width_wide = jnp.pad(width_wide, ((0, spare), (0, 0)))
    height_wide = jnp.broadcast_to(height_rows[:, :, None], (plan.per, rank_x, rank_y))
    height_wide = jnp.pad(height_wide.reshape(plan.per, rank_x * rank_y, 1), ((0, 0), (0, spare), (0, 0)))
    table = height_wide * width_wide[None]
    core_part, height_part, width_part, back = pl.pallas_call(
        functools.partial(
            owner_kernel, plan=plan, batch=batch, rank_in=rank_in, rank_out=rank_out, modes=modes
        ),
        out_shape=[
            jax.ShapeDtypeStruct((2 * rank_in * pad_out, pairs), f32),
            jax.ShapeDtypeStruct((plan.per, pairs, 1), f32),
            jax.ShapeDtypeStruct((pairs, plane), f32),
            jax.ShapeDtypeStruct((2, rows, lanes), bf16),
        ],
        scratch_shapes=[
            pltpu.VMEM((2 * rank_in * pad_out, plane), f32),
            pltpu.VMEM((2 * rank_in * pad_out, plane), bf16),
            pltpu.VMEM((2 * rank_in * pad_out, plane), bf16),
            pltpu.VMEM((2, rows, lanes), f32),
        ],
        compiler_params=pltpu.CompilerParams(vmem_limit_bytes=VMEM_LIMIT),
    )(keep, core, jnp.swapaxes(core, 1, 2), table, height_wide, width_wide, *arrived)
    height_part = height_part[:, : rank_x * rank_y, 0].reshape(plan.per, rank_x, rank_y).sum(axis=2)
    width_part = width_part[: rank_x * rank_y, :modes].reshape(rank_x, rank_y, modes).sum(axis=0)
    return core_part, height_part, width_part, back


def exchange_sum(plan, bits, value):
    terms = [value.astype(f32)]
    for part in range(1, 1 << len(bits)):
        mask = sum(1 << bit for place, bit in enumerate(bits) if part >> place & 1)
        terms.append(plan.trade(value, mask).astype(f32))
    while len(terms) > 1:
        terms = [one + other for one, other in zip(terms[::2], terms[1::2])]
    return terms[0]


def all_reduce(plan, bits, value):
    for bit in bits:
        value = exchange_sum(plan, [bit], value)
    return value


def all_reduce_large(plan, me, value):
    split = []
    bits = list(range(plan.total.bit_length() - 1))
    for bit in bits[:3]:
        middle = value.shape[0] // 2
        high = (me >> bit) & 1
        keep = lax.dynamic_slice_in_dim(value, high * middle, middle, 0)
        send = lax.dynamic_slice_in_dim(value, (1 - high) * middle, middle, 0).astype(bf16)
        value = keep + plan.swap(send, bit).astype(f32)
        split.append((bit, high))
    for bit in bits[3:]:
        value = exchange_sum(plan, [bit], value.astype(bf16))
    value = value.astype(bf16)
    for bit, high in reversed(split):
        other = plan.swap(value, bit)
        value = jnp.where(
            high == 0, jnp.concatenate([value, other], axis=0), jnp.concatenate([other, value], axis=0)
        )
    return value.astype(f32)


def on_device(inputs, cotangent, input_factor, output_factor, height_factor, width_factor, core_tensor):
    batch, channels, rows_here, width = inputs.shape
    kept, rank_x = height_factor.shape
    modes, rank_y = width_factor.shape
    rank_in, rank_out = input_factor.shape[1], output_factor.shape[1]
    shards, blocks = lax.axis_size("sp"), lax.axis_size("ch")
    shard = lax.axis_index("sp")
    me = shard * blocks + lax.axis_index("ch")
    plan = Plan(shards * blocks, kept)
    table = row_tables(batch, width, modes)
    forth, back = column_tables(plan, kept, rows_here, rows_here * shards, me, shard)

    def padded(factor):
        rank = factor.shape[1]
        return jnp.pad(factor.T, ((0, round_up(rank, 8) - rank), (0, 0)))

    def exchanged(parts):
        total = first_exchange(plan, *parts)
        return total.reshape(2, total.shape[0] // 2, total.shape[1])

    rows_input, *left = forward(plan, inputs, table, padded(input_factor), forth, rank_in, modes)
    left = exchanged(left)
    rows_cot, *right = forward(plan, cotangent, table, padded(output_factor), forth, rank_out, modes)
    right = exchanged(right)
    keep, arrived, (core_tensor, height_factor, width_factor) = reduce_scatter(
        plan, (left, right), (core_tensor, height_factor, width_factor)
    )

    owner = me & (plan.owners - 1)
    height_rows = height_factor[jnp.arange(plan.per) * plan.owners + owner]
    core_part, height_part, width_part, back_parts = owner_work(
        plan, keep, arrived, core_tensor, height_rows, width_factor, batch
    )
    pieces = all_gather(plan, back_parts)

    counts = (me >> plan.halvings) == 0
    height_full = jnp.zeros((plan.per, plan.owners, rank_x), f32)
    height_full = lax.dynamic_update_slice(height_full, height_part[:, None], (0, owner, 0)).reshape(kept, rank_x)
    small = jnp.concatenate([height_full.T, width_part], axis=0)
    core_rows, core_lanes = core_part.shape
    total_rows = round_up(core_rows + small.shape[0], 64)
    wide_lanes = max(core_lanes, small.shape[1])
    summed = jnp.concatenate(
        [
            jnp.pad(core_part, ((0, 0), (0, wide_lanes - core_lanes))),
            jnp.pad(small, ((0, total_rows - core_rows - small.shape[0]), (0, wide_lanes - small.shape[1]))),
        ],
        axis=0,
    )
    summed = all_reduce_large(plan, me, jnp.where(counts, summed, 0.0))
    core_grad = summed[:core_rows].reshape(2, rank_in, -1, wide_lanes)[:, :, :rank_out, : rank_x * rank_y]
    core_grad = core_grad.reshape(core_tensor.shape)
    height_grad = summed[core_rows : core_rows + rank_x, :kept].T
    width_grad = summed[core_rows + rank_x : core_rows + rank_x + rank_y, :modes].T

    both = backward(plan, pieces, rows_input, rows_cot, back, (rank_in, rank_out), rows_here, modes)
    both = all_reduce(plan, range(blocks.bit_length() - 1, plan.total.bit_length() - 1), both)
    return (core_grad, both[:channels, :rank_in], both[channels:, :rank_out], height_grad, width_grad)


def solution(mesh):
    placed = (
        P(None, "ch", "sp", None),
        P(None, "ch", "sp", None),
        P("ch", None),
        P("ch", None),
        P(),
        P(),
        P(),
    )
    return jax.shard_map(
        on_device,
        mesh=mesh,
        in_specs=placed,
        out_specs=(P(), P("ch", None), P("ch", None), P(), P()),
        check_vma=False,
    )
```

```python
import functools
import math

import jax
import jax.numpy as jnp
import numpy as np
from jax import lax
from jax.experimental import pallas as pl
from jax.experimental.pallas import tpu as pltpu
from jax.sharding import PartitionSpec as P


f32 = jnp.float32
bf16 = jnp.bfloat16
AXES = ("sp", "ch")
LANE = 128
VMEM_LIMIT = 60 * 1024 * 1024


def round_up(value, unit):
    return -(-value // unit) * unit


def row_tables(batch, width, modes):
    phases = (np.arange(width)[:, None] * np.arange(modes)[None, :] % width).astype(np.float32)
    angles = phases * np.float32(2.0 * math.pi / width)
    scaling = np.float32(1.0 / math.sqrt(width))
    table = np.concatenate([np.cos(angles) * scaling, -np.sin(angles) * scaling], axis=1)
    base = jnp.asarray(table, dtype=bf16)
    span = 2 * modes
    reach = max(round_up(b * span % LANE + span, LANE) for b in range(batch))
    starts = [b * span % LANE for b in range(batch)]
    return jnp.stack([jnp.pad(base, ((0, 0), (start, reach - start - span))) for start in starts])


class Plan:
    def __init__(self, total, kept):
        bits = total.bit_length() - 1
        self.total = total
        self.halvings = 0
        while self.halvings < bits and kept % (2 << self.halvings) == 0:
            self.halvings += 1
        self.owners = 1 << self.halvings
        self.per = kept // self.owners
        first = list(range(self.halvings))
        second = list(first)
        if self.halvings > 2:
            second[1], second[2] = second[2], second[1]
        self.orders = (first, second)
        self.early = tuple([order[1], order[0]] + order[2:] for order in self.orders)
        self.rest = list(range(self.halvings, bits))
        self.turns = [[turn] for turn in range(self.halvings)]

    def flips(self, order):
        masks = []
        for relative in range(self.owners):
            mask = 0
            for turn, bit in enumerate(order):
                if relative >> (self.halvings - 1 - turn) & 1:
                    mask |= 1 << bit
            masks.append(mask)
        return np.asarray(masks, dtype=np.int32)

    def masks(self, color, turn):
        bits = [self.orders[color][t] for t in self.turns[turn]]
        return [
            sum(1 << bit for place, bit in enumerate(bits) if part >> (len(bits) - 1 - place) & 1)
            for part in range(1, 1 << len(bits))
        ]

    def trade(self, value, mask):
        return lax.ppermute(value, AXES, [(i, i ^ mask) for i in range(self.total)])

    def swap(self, value, bit):
        return self.trade(value, 1 << bit)


def two_exchanges(plan, orders, keep, *sends):
    middle = keep.shape[0] // 2
    keeps = [keep[:middle], keep[middle:]]
    for turn in range(2):
        bits = [order[turn] for order in orders]
        if turn > 0:
            middle = middle // 2
            sends = [total[middle:].astype(bf16) for total in keeps]
            keeps = [total[:middle] for total in keeps]
        if bits[0] == bits[1] and turn > 0:
            both = plan.swap(jnp.concatenate(sends, axis=0), bits[0])
            arrived = [both[:middle], both[middle:]]
        else:
            arrived = [plan.swap(part, bit) for part, bit in zip(sends, bits)]
        keeps = [part + other.astype(f32) for part, other in zip(keeps, arrived)]
    return keeps


def reduce_scatter(plan, fields, late):
    keeps = [jnp.stack([field[color] for field in fields]) for color in range(2)]
    arrived = []
    for turn in range(2, len(plan.turns)):
        keeps = [sum([other[color].astype(f32) for other in arrived], keeps[color]) for color in range(2)]
        if turn == 2:
            keeps, late = lax.optimization_barrier((keeps, late))
        parts = 1 << len(plan.turns[turn])
        size = keeps[0].shape[1] // parts
        masks = [plan.masks(color, turn) for color in range(2)]
        arrived = []
        for part in range(1, parts):
            sends = [keep[:, part * size : (part + 1) * size].astype(bf16) for keep in keeps]
            if masks[0] == masks[1]:
                arrived.append(plan.trade(jnp.stack(sends), masks[0][part - 1]))
            else:
                arrived.append([plan.trade(sends[color], masks[color][part - 1]) for color in range(2)])
        keeps = [keep[:, :size] for keep in keeps]
    keep = jnp.stack(keeps)
    arrived = [other if isinstance(other, jax.Array) else jnp.stack(other) for other in arrived]
    for bit in plan.rest:
        value = sum([other.astype(f32) for other in arrived], keep).astype(bf16)
        keep, arrived = value.astype(f32), [plan.swap(value, bit)]
    return keep, arrived, late


def all_gather(plan, both):
    values = None
    for turn in reversed(range(len(plan.turns))):
        masks = [plan.masks(color, turn) for color in range(2)]
        if values is None:
            if masks[0] == masks[1]:
                others = [plan.trade(both, mask) for mask in masks[0]]
            else:
                others = list(zip(*[[plan.trade(both[color], mask) for mask in masks[color]] for color in range(2)]))
            values = [both[0], both[1]]
        else:
            values = [jnp.concatenate([values[color]] + [o[color] for o in others], axis=0) for color in range(2)]
            if masks[0] == masks[1] and turn > 0:
                both = jnp.stack(values)
                others = [plan.trade(both, mask) for mask in masks[0]]
                continue
            if turn == 0:
                values = lax.optimization_barrier(values)
            others = list(zip(*[[plan.trade(values[color], mask) for mask in masks[color]] for color in range(2)]))
    return [values[0], others[0][0], values[1], others[0][1]]


def column_tables(plan, orders, kept, rows_here, height, me, shard):
    owner = me & (plan.owners - 1)
    heights = shard * rows_here + jnp.arange(rows_here, dtype=jnp.int32)
    flips = jnp.asarray(np.stack([plan.flips(order) for order in orders]))
    owned = jnp.bitwise_xor(owner, flips)
    ordinal = jnp.arange(plan.per, dtype=jnp.int32)[None, :, None] * plan.owners + owned[:, None, :]
    ordinal = ordinal.reshape(2, kept)
    frequency = jnp.where(ordinal < kept // 2, ordinal, ordinal + (height - kept))
    phases = (frequency[:, :, None] * heights[None, None, :] % height).astype(f32)
    angles = phases * (2.0 * math.pi / height)
    scaling = 1.0 / math.sqrt(height)
    cosine = (jnp.cos(angles) * scaling).astype(bf16)
    sines = (jnp.sin(angles) * scaling).astype(bf16)
    forth = jnp.concatenate([cosine, sines], axis=1)
    back = jnp.concatenate([jnp.swapaxes(cosine, 1, 2), jnp.swapaxes(sines, 1, 2)], axis=1)
    return forth, back


def turned(value, modes, sign):
    lanes = value.shape[1]
    lane = lax.broadcasted_iota(jnp.int32, value.shape, 1)
    even = (lane // modes) % 2 == 0
    ahead = pltpu.roll(value, lanes - modes, 1)
    behind = pltpu.roll(value, modes, 1)
    if sign > 0:
        return jnp.where(even, ahead, -behind)
    return jnp.where(even, -ahead, behind)


def forward_kernel(
    x_ref, table_ref, factor_ref, forth_ref, rows_ref, keep_ref, send0_ref, send1_ref,
    raw, projected, packed, *, plan, rank, rows_here,
):
    step = pl.program_id(0)
    batch, channels, block, width = x_ref.shape
    lanes = keep_ref.shape[1]
    span = lanes // batch
    modes = span // 2
    tiles = lanes // LANE
    kept = plan.per * plan.owners
    half = rank // 2
    rank_pad = factor_ref.shape[0]
    segment = packed.shape[1] // (2 * plan.owners)
    reach = table_ref.shape[2] // LANE
    gap = block + 8
    some = max(1, 256 // block)
    for b in range(batch):
        for first in range(0, channels, some):
            values = jnp.dot(
                x_ref[b, first : first + some].reshape(some * block, width), table_ref[b], preferred_element_type=f32
            )
            for t in range(reach):
                for i in range(some):
                    raw[b * reach + t, (first + i) * gap : (first + i) * gap + block] = values[
                        i * block : (i + 1) * block, t * LANE : (t + 1) * LANE
                    ]
    for h in range(block):
        parts = [None] * tiles
        for b in range(batch):
            for t in range(reach):
                place = b * span // LANE + t
                if place < tiles:
                    piece = raw[b * reach + t, pl.ds(h, channels, stride=gap), :]
                    parts[place] = piece if parts[place] is None else parts[place] + piece
        joined = jnp.concatenate(parts, axis=1).astype(bf16)
        rows_ref[:, h * lanes : (h + 1) * lanes] = joined
        mixed = jnp.dot(factor_ref[...], joined, preferred_element_type=f32)
        for t in range(tiles):
            projected[t, pl.ds(step * block + h, rank_pad, stride=rows_here + 8), :] = mixed[:, t * LANE : (t + 1) * LANE]

    @pl.when(step == pl.num_programs(0) - 1)
    def _():
        if segment > plan.per * half:
            for color in range(2):
                for spare in range(plan.per * half, segment):
                    for t in range(tiles):
                        packed[t, pl.ds(color * plan.owners * segment + spare, plan.owners, stride=segment), :] = (
                            jnp.zeros((plan.owners, LANE), f32)
                        )
        for color in range(2):

            @pl.loop(0, half, unroll=True)
            def _(a):
                start = pl.multiple_of((color * half + a) * (rows_here + 8), 8)
                plane = jnp.concatenate(
                    [projected[t, pl.ds(start, rows_here), :] for t in range(tiles)], axis=1
                ).astype(bf16)
                both = jnp.dot(forth_ref[color], plane, preferred_element_type=f32)
                spectrum = both[:kept] + turned(both[kept:], modes, 1)
                for j in range(plan.per):
                    for t in range(tiles):
                        packed[
                            t, pl.ds(color * plan.owners * segment + j * half + a, plan.owners, stride=segment), :
                        ] = spectrum[j * plan.owners : (j + 1) * plan.owners, t * LANE : (t + 1) * LANE]

        middle = keep_ref.shape[0] // 2
        for t in range(tiles):
            for color, send_ref in enumerate((send0_ref, send1_ref)):
                here, start = slice(color * middle, (color + 1) * middle), 2 * color * middle
                keep_ref[here, t * LANE : (t + 1) * LANE] = packed[t, start : start + middle]
                send_ref[:, t * LANE : (t + 1) * LANE] = packed[t, start + middle : start + 2 * middle].astype(bf16)


def forward(plan, field, table, factor, forth, rank, modes):
    batch, channels, rows_here, width = field.shape
    span = 2 * modes
    lanes = batch * span
    kept = plan.per * plan.owners
    block = min(16, rows_here)
    segment = round_up(plan.per * rank // 2, 8)
    rank_pad = factor.shape[0]
    middle = plan.owners * segment // 2
    return pl.pallas_call(
        functools.partial(forward_kernel, plan=plan, rank=rank, rows_here=rows_here),
        grid=(rows_here // block,),
        in_specs=[
            pl.BlockSpec((batch, channels, block, width), lambda s: (0, 0, s, 0)),
            pl.BlockSpec(table.shape, lambda s: (0, 0, 0)),
            pl.BlockSpec((rank_pad, channels), lambda s: (0, 0)),
            pl.BlockSpec((2, 2 * kept, rows_here), lambda s: (0, 0, 0)),
        ],
        out_specs=[
            pl.BlockSpec((channels, block * lanes), lambda s: (0, s)),
        ]
        + [pl.BlockSpec((rows, lanes), lambda s: (0, 0)) for rows in (2 * middle, middle, middle)],
        out_shape=[
            jax.ShapeDtypeStruct((channels, rows_here * lanes), bf16),
        ]
        + [jax.ShapeDtypeStruct((2 * middle, lanes), f32)]
        + [jax.ShapeDtypeStruct((middle, lanes), bf16)] * 2,
        scratch_shapes=[
            pltpu.VMEM((batch * table.shape[2] // LANE, channels * (block + 8), LANE), f32),
            pltpu.VMEM((lanes // LANE, rank_pad * (rows_here + 8), LANE), f32),
            pltpu.VMEM((lanes // LANE, 2 * plan.owners * segment, LANE), f32),
        ],
        compiler_params=pltpu.CompilerParams(vmem_limit_bytes=VMEM_LIMIT),
        cost_estimate=pl.CostEstimate(
            flops=2 * batch * channels * rows_here * width * span,
            bytes_accessed=2 * batch * channels * rows_here * (width + span),
            transcendentals=0,
        ),
    )(field, table, factor, forth)


def backward_kernel(
    g00_ref, g01_ref, g10_ref, g11_ref, rows_in_ref, rows_out_ref, back_ref, out_ref,
    wide, grids_in, grids_out, block_in, block_out, *, plan, ranks, rows_here, modes,
):
    step = pl.program_id(0)
    tiles = wide.shape[0]
    lanes = tiles * LANE
    segments = [round_up(plan.per * rank // 2, 8) for rank in ranks]
    used = sum(segments)
    stride = used + (8 if used // 8 % 2 == 0 else 16)
    channels = rows_in_ref.shape[0]

    @pl.when(step == 0)
    def _():
        out_ref[...] = jnp.zeros_like(out_ref)
        for grids, rank in zip((grids_in, grids_out), ranks):
            spare = grids.shape[1] - rank * (rows_here + 8)
            if spare:
                grids[:, rank * (rows_here + 8) :, :] = jnp.zeros((tiles, spare, LANE), f32)
        for color, (one, other) in enumerate(((g00_ref, g01_ref), (g10_ref, g11_ref))):
            for t in range(tiles):
                for relative in range(plan.owners):
                    piece = one if relative < plan.owners // 2 else other
                    start = relative % (plan.owners // 2) * used
                    wide[t, relative * stride : relative * stride + used, :] = piece[
                        start : start + used, t * LANE : (t + 1) * LANE
                    ].astype(f32)
            for side, (grids, rank) in enumerate(zip((grids_in, grids_out), ranks)):
                half = rank // 2
                base = side * segments[0]

                @pl.loop(0, half, unroll=True)
                def _(a):
                    spectrum = jnp.concatenate(
                        [
                            jnp.concatenate(
                                [
                                    wide[t, pl.ds(base + j * half + a, plan.owners, stride=stride), :]
                                    for t in range(tiles)
                                ],
                                axis=1,
                            )
                            for j in range(plan.per)
                        ],
                        axis=0,
                    ).astype(bf16)
                    both = jnp.dot(back_ref[color], spectrum, preferred_element_type=f32)
                    start = pl.multiple_of((color * half + a) * (rows_here + 8), 8)
                    grid = both[:rows_here] + turned(both[rows_here:], modes, -1)
                    for t in range(tiles):
                        grids[t, pl.ds(start, rows_here), :] = grid[:, t * LANE : (t + 1) * LANE]

    for side, (grids, block_ref, rows_ref) in enumerate(
        ((grids_in, block_in, rows_in_ref), (grids_out, block_out, rows_out_ref))
    ):
        for h in range(block_ref.shape[1] // lanes):
            for t in range(tiles):
                block_ref[:, h * lanes + t * LANE : h * lanes + (t + 1) * LANE] = grids[
                    t, pl.ds(step * (block_ref.shape[1] // lanes) + h, block_ref.shape[0], stride=rows_here + 8), :
                ].astype(bf16)
        out_ref[side * channels : (side + 1) * channels, : block_ref.shape[0]] += lax.dot_general(
            rows_ref[...], block_ref[...], (((1,), (1,)), ((), ())), preferred_element_type=f32
        )


def backward(plan, pieces, rows_in, rows_out, back, ranks, rows_here, modes):
    channels = rows_in.shape[0]
    lanes = rows_in.shape[1] // rows_here
    block = min(16, rows_here)
    pads = [round_up(rank, 8) for rank in ranks]
    whole = lambda s: (0, 0)
    part = pl.BlockSpec((channels, block * lanes), lambda s: (0, s))
    return pl.pallas_call(
        functools.partial(backward_kernel, plan=plan, ranks=ranks, rows_here=rows_here, modes=modes),
        grid=(rows_here // block,),
        in_specs=[pl.BlockSpec(piece.shape, whole) for piece in pieces]
        + [part, part, pl.BlockSpec(back.shape, lambda s: (0, 0, 0))],
        out_specs=pl.BlockSpec((2 * channels, max(pads)), whole),
        out_shape=jax.ShapeDtypeStruct((2 * channels, max(pads)), f32),
        scratch_shapes=[pltpu.VMEM((lanes // LANE, 2 * pieces[0].shape[0] + 16 * plan.owners, LANE), f32)]
        + [pltpu.VMEM((lanes // LANE, pad * (rows_here + 8), LANE), f32) for pad in pads]
        + [pltpu.VMEM((pad, block * lanes), bf16) for pad in pads],
        compiler_params=pltpu.CompilerParams(vmem_limit_bytes=VMEM_LIMIT),
        cost_estimate=pl.CostEstimate(
            flops=2 * channels * sum(pads) * rows_here * lanes,
            bytes_accessed=4 * channels * rows_here * lanes,
            transcendentals=0,
        ),
    )(*pieces, rows_in, rows_out, back)


def owner_kernel(
    keep_ref, core_ref, core_t_ref, modes_ref, height_ref, width_ref, *refs, plan, batch, rank_in, rank_out, modes,
):
    pad_in, pad_out = round_up(rank_in, 8), round_up(rank_out, 8)
    lanes = keep_ref.shape[3]
    plane = modes_ref.shape[2]
    segment_in = keep_ref.shape[2]
    *arrived, core_out, height_out, width_out, back_ref, modal, pair, pair_low, returned = refs
    sums = [sum([ref[:, side].astype(f32) for ref in arrived], keep_ref[:, side]) for side in range(2)]
    rows = rank_in * pad_out

    def gathered(sums, j, rank, pad):
        half = rank // 2
        parts = [sums[color, j * half : (j + 1) * half] for color in range(2)]
        if pad > rank:
            parts.append(jnp.zeros((pad - rank, lanes), f32))
        joined = jnp.concatenate(parts, axis=0)
        pieces = []
        for n in range(2 * batch):
            turned_by = (lanes - n * modes) % lanes
            piece = pltpu.roll(joined, turned_by, 1) if turned_by else joined
            pieces.append(piece[:, :plane])
        return pieces

    lane = lax.broadcasted_iota(jnp.int32, (1, plane), 1) < modes

    def spread(pieces):
        total = None
        for n, piece in enumerate(pieces):
            kept = jnp.where(lane, piece, 0.0)
            wide = jnp.concatenate([kept, jnp.zeros((kept.shape[0], lanes - plane), f32)], axis=1)
            wide = pltpu.roll(wide, n * modes, 1) if n else wide
            total = wide if total is None else total + wide
        return total

    core_sum = None
    width_sum = None
    for j in range(plan.per):
        left = gathered(sums[0], j, rank_in, pad_in)
        right = gathered(sums[1], j, rank_out, pad_out)
        table = modes_ref[j].astype(bf16)
        table_low = (modes_ref[j] - table.astype(f32)).astype(bf16)
        modal[...] = (
            jnp.dot(core_ref[0], table, preferred_element_type=f32)
            + jnp.dot(core_ref[1], table, preferred_element_type=f32)
            + jnp.dot(core_ref[0], table_low, preferred_element_type=f32)
        )
        inward = [[] for _ in range(2 * batch)]
        outward = [jnp.zeros((pad_out, plane), f32) for _ in range(2 * batch)]
        for a in range(rank_in):
            modal_real = modal[a * pad_out : (a + 1) * pad_out]
            modal_imag = modal[rows + a * pad_out : rows + (a + 1) * pad_out]
            pair_real = jnp.zeros((pad_out, plane), f32)
            pair_imag = jnp.zeros((pad_out, plane), f32)
            for b in range(batch):
                left_real = left[2 * b][a : a + 1]
                left_imag = -left[2 * b + 1][a : a + 1]
                right_real = right[2 * b]
                right_imag = right[2 * b + 1]
                pair_real += left_real * right_real - left_imag * right_imag
                pair_imag += left_real * right_imag + left_imag * right_real
                inward[2 * b].append(
                    jnp.sum(modal_real * right_real + modal_imag * right_imag, axis=0, keepdims=True)
                )
                inward[2 * b + 1].append(
                    jnp.sum(modal_real * right_imag - modal_imag * right_real, axis=0, keepdims=True)
                )
                outward[2 * b] += modal_real * left_real + modal_imag * left_imag
                outward[2 * b + 1] -= modal_real * left_imag - modal_imag * left_real
            for start, value in ((a * pad_out, pair_real), (rows + a * pad_out, pair_imag)):
                high = value.astype(bf16)
                pair[start : start + pad_out] = high
                pair_low[start : start + pad_out] = (value - high.astype(f32)).astype(bf16)
        contract = (((1,), (1,)), ((), ()))
        part = (
            lax.dot_general(pair[...], table, contract, preferred_element_type=f32)
            + lax.dot_general(pair_low[...], table, contract, preferred_element_type=f32)
            + lax.dot_general(pair[...], table_low, contract, preferred_element_type=f32)
        )
        core_sum = part if j == 0 else core_out[...] + part
        core_out[...] = core_sum
        terms = (
            jnp.dot(core_t_ref[0], pair[...], preferred_element_type=f32)
            + jnp.dot(core_t_ref[1], pair[...], preferred_element_type=f32)
            + jnp.dot(core_t_ref[0], pair_low[...], preferred_element_type=f32)
        )
        height_out[j] = jnp.sum(terms * width_ref[...], axis=1, keepdims=True)
        by_width = terms * height_ref[j]
        width_sum = by_width if j == 0 else width_sum + by_width
        half_in, half_out = rank_in // 2, rank_out // 2
        inward_all = spread([jnp.concatenate(rows_of, axis=0) for rows_of in inward])
        outward_all = spread(outward)
        for color in range(2):
            returned[color, j * half_in : (j + 1) * half_in] = inward_all[color * half_in : (color + 1) * half_in]
            returned[color, segment_in + j * half_out : segment_in + (j + 1) * half_out] = outward_all[
                color * half_out : (color + 1) * half_out
            ]
    for color in range(2):
        for start, used, stop in (
            (0, plan.per * rank_in // 2, segment_in),
            (segment_in, plan.per * rank_out // 2, returned.shape[1]),
        ):
            if start + used < stop:
                returned[color, start + used : stop] = jnp.zeros((stop - start - used, lanes), f32)
    back_ref[...] = returned[...].astype(bf16)
    width_out[...] = width_sum


def owner_work(plan, keep, arrived, core_tensor, height_rows, width_factor, batch):
    _, rank_in, rank_out, rank_x, rank_y = core_tensor.shape
    modes = width_factor.shape[0]
    pad_out = round_up(rank_out, 8)
    pairs = round_up(rank_x * rank_y, 8)
    plane = round_up(modes, 128)
    lanes = keep.shape[3]
    rows = 2 * keep.shape[2]
    spare = pairs - rank_x * rank_y
    core = core_tensor.reshape(2, rank_in, rank_out, rank_x * rank_y)
    core = jnp.pad(core, ((0, 0), (0, 0), (0, pad_out - rank_out), (0, spare)))
    core = core.reshape(2 * rank_in * pad_out, pairs)
    core_high = core.astype(bf16)
    core = jnp.stack([core_high, (core - core_high.astype(f32)).astype(bf16)])
    width_turned = jnp.pad(width_factor.T, ((0, 0), (0, plane - modes)))
    width_wide = jnp.broadcast_to(width_turned[None], (rank_x, rank_y, plane)).reshape(rank_x * rank_y, plane)
    width_wide = jnp.pad(width_wide, ((0, spare), (0, 0)))
    height_wide = jnp.broadcast_to(height_rows[:, :, None], (plan.per, rank_x, rank_y))
    height_wide = jnp.pad(height_wide.reshape(plan.per, rank_x * rank_y, 1), ((0, 0), (0, spare), (0, 0)))
    table = height_wide * width_wide[None]
    core_part, height_part, width_part, back = pl.pallas_call(
        functools.partial(
            owner_kernel, plan=plan, batch=batch, rank_in=rank_in, rank_out=rank_out, modes=modes
        ),
        out_shape=[
            jax.ShapeDtypeStruct((2 * rank_in * pad_out, pairs), f32),
            jax.ShapeDtypeStruct((plan.per, pairs, 1), f32),
            jax.ShapeDtypeStruct((pairs, plane), f32),
            jax.ShapeDtypeStruct((2, rows, lanes), bf16),
        ],
        scratch_shapes=[
            pltpu.VMEM((2 * rank_in * pad_out, plane), f32),
            pltpu.VMEM((2 * rank_in * pad_out, plane), bf16),
            pltpu.VMEM((2 * rank_in * pad_out, plane), bf16),
            pltpu.VMEM((2, rows, lanes), f32),
        ],
        compiler_params=pltpu.CompilerParams(vmem_limit_bytes=VMEM_LIMIT),
    )(keep, core, jnp.swapaxes(core, 1, 2), table, height_wide, width_wide, *arrived)
    height_part = height_part[:, : rank_x * rank_y, 0].reshape(plan.per, rank_x, rank_y).sum(axis=2)
    width_part = width_part[: rank_x * rank_y, :modes].reshape(rank_x, rank_y, modes).sum(axis=0)
    return core_part, height_part, width_part, back


def exchange_sum(plan, bits, value):
    terms = [value.astype(f32)]
    for part in range(1, 1 << len(bits)):
        mask = sum(1 << bit for place, bit in enumerate(bits) if part >> place & 1)
        terms.append(plan.trade(value, mask).astype(f32))
    while len(terms) > 1:
        terms = [one + other for one, other in zip(terms[::2], terms[1::2])]
    return terms[0]


def all_reduce(plan, bits, value):
    for bit in bits:
        value = exchange_sum(plan, [bit], value)
    return value


def all_reduce_large(plan, me, value):
    split = []
    bits = list(range(plan.total.bit_length() - 1))
    for bit in bits[:3]:
        middle = value.shape[0] // 2
        high = (me >> bit) & 1
        keep = lax.dynamic_slice_in_dim(value, high * middle, middle, 0)
        send = lax.dynamic_slice_in_dim(value, (1 - high) * middle, middle, 0).astype(bf16)
        value = keep + plan.swap(send, bit).astype(f32)
        split.append((bit, high))
    for bit in bits[3:]:
        value = exchange_sum(plan, [bit], value.astype(bf16))
    value = value.astype(bf16)
    for bit, high in reversed(split):
        other = plan.swap(value, bit)
        value = jnp.where(
            high == 0, jnp.concatenate([value, other], axis=0), jnp.concatenate([other, value], axis=0)
        )
    return value.astype(f32)


def on_device(inputs, cotangent, input_factor, output_factor, height_factor, width_factor, core_tensor):
    batch, channels, rows_here, width = inputs.shape
    kept, rank_x = height_factor.shape
    modes, rank_y = width_factor.shape
    rank_in, rank_out = input_factor.shape[1], output_factor.shape[1]
    shards, blocks = lax.axis_size("sp"), lax.axis_size("ch")
    shard = lax.axis_index("sp")
    me = shard * blocks + lax.axis_index("ch")
    plan = Plan(shards * blocks, kept)
    table = row_tables(batch, width, modes)
    early, _ = column_tables(plan, plan.early, kept, rows_here, rows_here * shards, me, shard)
    forth, back = column_tables(plan, plan.orders, kept, rows_here, rows_here * shards, me, shard)

    def padded(factor):
        rank = factor.shape[1]
        return jnp.pad(factor.T, ((0, round_up(rank, 8) - rank), (0, 0)))

    rows_input, *left = forward(plan, inputs, table, padded(input_factor), early, rank_in, modes)
    left = two_exchanges(plan, plan.early, *left)
    rows_cot, *right = forward(plan, cotangent, table, padded(output_factor), forth, rank_out, modes)
    right = two_exchanges(plan, plan.orders, *right)
    keep, arrived, (core_tensor, height_factor, width_factor) = reduce_scatter(
        plan, (left, right), (core_tensor, height_factor, width_factor)
    )

    owner = me & (plan.owners - 1)
    height_rows = height_factor[jnp.arange(plan.per) * plan.owners + owner]
    core_part, height_part, width_part, back_parts = owner_work(
        plan, keep, arrived, core_tensor, height_rows, width_factor, batch
    )
    pieces = all_gather(plan, back_parts)

    counts = (me >> plan.halvings) == 0
    height_full = jnp.zeros((plan.per, plan.owners, rank_x), f32)
    height_full = lax.dynamic_update_slice(height_full, height_part[:, None], (0, owner, 0)).reshape(kept, rank_x)
    small = jnp.concatenate([height_full.T, width_part], axis=0)
    core_rows, core_lanes = core_part.shape
    total_rows = round_up(core_rows + small.shape[0], 64)
    wide_lanes = max(core_lanes, small.shape[1])
    summed = jnp.concatenate(
        [
            jnp.pad(core_part, ((0, 0), (0, wide_lanes - core_lanes))),
            jnp.pad(small, ((0, total_rows - core_rows - small.shape[0]), (0, wide_lanes - small.shape[1]))),
        ],
        axis=0,
    )
    summed = all_reduce_large(plan, me, jnp.where(counts, summed, 0.0))
    core_grad = summed[:core_rows].reshape(2, rank_in, -1, wide_lanes)[:, :, :rank_out, : rank_x * rank_y]
    core_grad = core_grad.reshape(core_tensor.shape)
    height_grad = summed[core_rows : core_rows + rank_x, :kept].T
    width_grad = summed[core_rows + rank_x : core_rows + rank_x + rank_y, :modes].T

    both = backward(plan, pieces, rows_input, rows_cot, back, (rank_in, rank_out), rows_here, modes)
    both = all_reduce(plan, range(blocks.bit_length() - 1, plan.total.bit_length() - 1), both)
    return (core_grad, both[:channels, :rank_in], both[channels:, :rank_out], height_grad, width_grad)


def solution(mesh):
    placed = (
        P(None, "ch", "sp", None),
        P(None, "ch", "sp", None),
        P("ch", None),
        P("ch", None),
        P(),
        P(),
        P(),
    )
    return jax.shard_map(
        on_device,
        mesh=mesh,
        in_specs=placed,
        out_specs=(P(), P("ch", None), P("ch", None), P(), P()),
        check_vma=False,
    )
```
